32 devices in a mesh: row: 4 (over z), col: 4 (over y, x), layer: 2 (over core).
Axes of the slice: x: 2, y: 2, z: 4, core: 2. Of those that a mesh axis runs over, the one named last changes fastest.
Arguments:
- stored_blocks: float32 [4, 4, 96, 128, 128], P('row', 'col'), as said below
- pattern: int32 [4, 4, 96], replicated, may hold values from -1 to 95, as said below
- result_cols: int32 [4, 4, 96, 2], P('row', 'col'), may hold values from 0 to 95, as said below
Outputs:
- result_blocks: float32 [4, 4, 96, 2, 128, 128], P('row', 'col', 'layer')
The draws below stay inside these ranges and needn't reach their ends.
Inputs may be any that keep to these rules, and one draw needn't show every extreme that they name: Each block row of a tile holds at most one block. The pattern is symmetric: pattern(i, j, r) = c exactly when pattern(j, i, c) = r. Diagonal tiles hold just the diagonal blocks: pattern(i, i, r) = r. `result_cols`: the 2 columns listed for one block row of a tile are distinct. X is symmetric. stored_blocks(i, j, r) holds the block at local row r and local column pattern(i, j, r) of tile (i, j) when that block is upper; every other slot is zero.
All inputs are finite; a program needn't handle non-finite values.
Results may differ from the reference program's by a relative error of at most 0.0003.
Values sent between devices are 32-bit elements; how exact they have to be, the bound alone decides.
No kernel may reach another device: no remote copies, remote signals or barrier semaphores. Data moves between devices by JAX's collectives and lax.ppermute only.
A program may use at most 128 MiB of HBM per device.

```python
import jax
import jax.numpy as jnp
from jax import lax

BS = 128
KR = 2
GRID = 4
BR = 96


def permute_rows(row_key):
    return jax.random.permutation(row_key, BR)


def block_pattern(key):
    pair_keys = jax.random.split(jax.random.fold_in(key, 17), GRID * GRID)
    orders = jax.vmap(permute_rows)(pair_keys).reshape(GRID, GRID, BR).astype(jnp.int32)
    inverse = jnp.argsort(orders, axis=-1).astype(jnp.int32)
    tile_row = jnp.arange(GRID)[:, None, None]
    tile_col = jnp.arange(GRID)[None, :, None]
    spacing = jnp.abs(tile_row - tile_col)
    distance = jnp.minimum(spacing, GRID - spacing)
    chance = jax.random.randint(jax.random.fold_in(key, 23), (GRID, GRID, BR), 0, 2 * GRID)
    kept = chance >= 2 * distance - 1
    inverse_swapped = jnp.swapaxes(inverse, 0, 1)
    kept_mirror = jnp.take_along_axis(jnp.swapaxes(kept, 0, 1), inverse_swapped, axis=-1)
    local_rows = jnp.broadcast_to(jnp.arange(BR, dtype=jnp.int32)[None, None, :], (GRID, GRID, BR))
    upper_cols = jnp.where(kept, orders, -1)
    lower_cols = jnp.where(kept_mirror, inverse_swapped, -1)
    chosen = jnp.where(tile_row == tile_col, local_rows, jnp.where(tile_row < tile_col, upper_cols, lower_cols))
    return chosen.astype(jnp.int32)


def draw_pattern(key, part):
    return block_pattern(key)


def draw_result_cols(key, part):
    pattern = block_pattern(key)
    tile_row = jnp.arange(GRID)[:, None, None]
    tile_col = jnp.arange(GRID)[None, :, None]
    local_rows = jnp.arange(BR)[None, None, :]
    spare_first = jax.random.randint(jax.random.fold_in(key, 31), (GRID, GRID, BR), 0, BR)
    first = jnp.where(pattern >= 0, pattern, spare_first)
    middle = jax.random.randint(jax.random.fold_in(key, 37), (GRID, GRID, BR), 0, GRID)
    step_cols = pattern[tile_row, middle, local_rows]
    reach = pattern[middle, tile_col, jnp.maximum(step_cols, 0)]
    valid = (step_cols >= 0) & (reach >= 0) & (reach != first)
    spare_second = (first + 1 + jax.random.randint(jax.random.fold_in(key, 41), (GRID, GRID, BR), 0, BR - 1)) % BR
    second = jnp.where(valid, reach, spare_second)
    return jnp.stack([first, second], axis=-1).astype(jnp.int32)


def draw_stored_blocks(key, part):
    pattern = block_pattern(key)
    safe_cols = jnp.maximum(pattern, 0)
    scale = BS ** (-0.25)
    raw = jax.random.normal(jax.random.fold_in(key, 53), (GRID, GRID, BR, BS, BS), jnp.float32) * scale
    gains = jnp.exp(0.1 * jax.random.normal(jax.random.fold_in(key, 59), (GRID, BR), jnp.float32))
    tile_row = jnp.arange(GRID)[:, None, None]
    tile_col = jnp.arange(GRID)[None, :, None]
    local_rows = jnp.arange(BR)[None, None, :]
    mirrored = jnp.swapaxes(jnp.swapaxes(raw, 0, 1)[tile_row, tile_col, safe_cols], -1, -2)
    symmetric = (raw + jnp.swapaxes(raw, -1, -2)) * 0.5 ** 0.5
    values = jnp.where((tile_row == tile_col)[..., None, None], symmetric, jnp.where((tile_row < tile_col)[..., None, None], raw, mirrored))
    row_gain = gains[tile_row, local_rows]
    col_gain = gains[jnp.broadcast_to(tile_col, (GRID, GRID, BR)), safe_cols]
    values = values * (row_gain * col_gain)[..., None, None]
    stored = (pattern >= 0) & (local_rows * GRID + tile_row <= safe_cols * GRID + tile_col)
    return jnp.where(stored[..., None, None], values, 0.0).astype(jnp.float32)


def setup_inputs(seed: int = 0) -> dict:
    streams_of = jax.random.split(jax.random.key(seed), 4)
    stored_blocks = draw_stored_blocks(jax.random.fold_in(streams_of[3], 71), 0)
    pattern = draw_pattern(jax.random.fold_in(streams_of[3], 71), 0)
    result_cols = draw_result_cols(jax.random.fold_in(streams_of[3], 71), 0)
    return {"stored_blocks": stored_blocks, "pattern": pattern, "result_cols": result_cols}


def complete_tiles(stored_blocks, pattern):
    tile_row = jnp.arange(GRID)[:, None, None]
    tile_col = jnp.arange(GRID)[None, :, None]
    local_rows = jnp.arange(BR)[None, None, :]
    safe_cols = jnp.maximum(pattern, 0)
    is_upper = local_rows * GRID + tile_row <= safe_cols * GRID + tile_col
    mirrored = jnp.swapaxes(jnp.swapaxes(stored_blocks, 0, 1)[tile_row, tile_col, safe_cols], -1, -2)
    return jnp.where(is_upper[..., None, None], stored_blocks, mirrored)


def accumulate(totals, left_tile, right_tile, left_cols, right_cols, wanted):
    inner_rows = jnp.maximum(left_cols, 0)
    partner = right_tile[inner_rows]
    target = right_cols[inner_rows]
    present = (left_cols >= 0) & (target >= 0)
    products = jnp.einsum("rab,rbc->rac", left_tile.astype(jnp.float32), partner.astype(jnp.float32), precision=lax.Precision.HIGHEST)
    matched = (present[:, None] & (wanted == target[:, None])).astype(jnp.float32)
    return totals + matched[:, :, None, None] * products[:, None]


def reference(stored_blocks, pattern, result_cols):
    full_tiles = complete_tiles(stored_blocks, pattern)

    def tile_product(flat):
        tile_row = flat // GRID
        tile_col = flat % GRID
        totals = jnp.zeros((BR, KR, BS, BS), jnp.float32)
        for middle in range(GRID):
            totals = accumulate(totals, full_tiles[tile_row, middle], full_tiles[middle, tile_col], pattern[tile_row, middle], pattern[middle, tile_col], result_cols[tile_row, tile_col])
        return totals

    summed = lax.map(tile_product, jnp.arange(GRID * GRID))
    return summed.reshape(GRID, GRID, BR, KR, BS, BS)
```

```python
import functools

import jax
import jax.numpy as jnp
from jax import lax
from jax.experimental import pallas as pl
from jax.experimental.pallas import tpu as pltpu
from jax.sharding import PartitionSpec as P

AXES = ("row", "col", "layer")
SMEM = functools.partial(pl.BlockSpec, memory_space=pltpu.SMEM)
VMEM = functools.partial(pl.BlockSpec, memory_space=pltpu.VMEM)


def shifted(value, axis, steps):
    count = lax.axis_size(axis)
    pairs = [(source, (source + steps) % count) for source in range(count)]
    return lax.ppermute(value, axis, pairs)


def accumulate(totals, left_tile, right_tile, left_cols, right_cols, wanted):
    inner_rows = jnp.maximum(left_cols, 0)
    partner = right_tile[inner_rows]
    target = right_cols[inner_rows]
    present = (left_cols >= 0) & (target >= 0)
    products = jnp.einsum(
        "rab,rbc->rac",
        left_tile,
        partner,
        precision=lax.Precision.HIGHEST,
        preferred_element_type=jnp.float32,
    )
    matched = (present[:, None] & (wanted == target[:, None])).astype(jnp.float32)
    return totals + matched[:, :, None, None] * products[:, None]


def complete(stored, mirror_source, pattern, tile_row, tile_col, grid_side):
    col_ids = pattern[tile_row, tile_col]
    safe_cols = jnp.maximum(col_ids, 0)
    local_rows = jnp.arange(stored.shape[0])
    is_upper = local_rows * grid_side + tile_row <= safe_cols * grid_side + tile_col
    mirrored = jnp.swapaxes(mirror_source[safe_cols], 1, 2)
    return jnp.where(is_upper[:, None, None], stored, mirrored)


def slow_path(own_tile, pattern, wanted):
    grid_side = lax.axis_size("row")
    layers = lax.axis_size("layer")
    my_row = lax.axis_index("row")
    my_col = lax.axis_index("col")
    my_layer = lax.axis_index("layer")
    row_count = own_tile.shape[0]
    half = row_count // layers
    mirror = send(own_tile, lambda i, j, l: (j, i, l))
    mirror = jnp.where(my_row == my_col, own_tile, mirror)
    mine = complete(own_tile, mirror, pattern, my_row, my_col, grid_side)
    first = my_layer * half
    mine_wanted = lax.dynamic_slice_in_dim(wanted, first, half)
    totals = jnp.zeros((half, wanted.shape[1]) + own_tile.shape[1:], jnp.float32)

    def step(middle, totals):
        def ring(axis, mine_at):
            def turn(_, held):
                tile, kept, at = held
                kept = jnp.where(at == middle, tile, kept)
                return shifted(tile, axis, -1), kept, (at + 1) % grid_side

            return lax.fori_loop(0, grid_side, turn, (mine, mine, mine_at))[1]

        left = lax.dynamic_slice_in_dim(ring("col", my_col), first, half)
        right = ring("row", my_row)
        left_cols = lax.dynamic_slice_in_dim(pattern[my_row, middle], first, half)
        return accumulate(totals, left, right, left_cols, pattern[middle, my_col], mine_wanted)

    return lax.fori_loop(0, grid_side, step, totals)


def send(value, target):
    rows, cols, layers = (lax.axis_size(axis) for axis in AXES)
    pairs = []
    for i in range(rows):
        for j in range(cols):
            for l in range(layers):
                to = target(i, j, l)
                if to is not None and to != (i, j, l):
                    pairs.append(
                        ((i * cols + j) * layers + l, (to[0] * cols + to[1]) * layers + to[2])
                    )
    return lax.ppermute(value, AXES, pairs)


def pick(table, index):
    ids = jnp.arange(table.shape[-1], dtype=jnp.int32)
    hit = index[..., :, None] == ids
    return jnp.sum(jnp.where(hit, table[..., None, :] + 1, 0), axis=-1) - 1


def ranks(mask):
    ids = jnp.arange(mask.shape[-1], dtype=jnp.int32)
    before = mask[..., None, :] & (ids[None, :] < ids[:, None])
    return jnp.sum(before.astype(jnp.int32), axis=-1)


def listing(mask, order, values, room, start=0):
    slots = jnp.arange(room, dtype=jnp.int32) + start
    hit = mask[..., None, :] & (order[..., None, :] == slots[:, None])
    return jnp.sum(jnp.where(hit, values[..., None, :], 0), axis=-1)


def upper_rows(cols, tile_row, tile_col, grid_side):
    ids = jnp.arange(cols.shape[-1], dtype=jnp.int32)
    return (cols >= 0) & (ids * grid_side + tile_row <= cols * grid_side + tile_col)


def split_dot(left, right, contract=((1,), (0,))):
    left_hi = left.astype(jnp.bfloat16)
    left_lo = (left - left_hi.astype(jnp.float32)).astype(jnp.bfloat16)
    right_hi = right.astype(jnp.bfloat16)
    right_lo = (right - right_hi.astype(jnp.float32)).astype(jnp.bfloat16)

    def dot(a, b):
        return lax.dot_general(a, b, (contract, ((), ())), preferred_element_type=jnp.float32)

    return dot(left_hi, right_hi) + (dot(left_hi, right_lo) + dot(left_lo, right_hi))


def ids2(shape, axis):
    return lax.broadcasted_iota(jnp.int32, shape, axis)


def pack_block(block):
    size = block.shape[0]
    half = size // 2
    shape = (half, size)
    low = pltpu.roll(block[half:], half, 1)
    packed = jnp.where(ids2(shape, 1) < ids2(shape, 0), low, block[:half])
    diagonal = jnp.sum(jnp.where(ids2(shape, 1) == ids2(shape, 0), low, 0.0), axis=0, keepdims=True)
    return packed, diagonal


def unpack_block(packed, diagonal):
    half, size = packed.shape
    shape = (size, size)
    both = jnp.concatenate([packed, pltpu.roll(packed, half, 1)], axis=0)
    turned = both.T
    row, lane = ids2(shape, 0), ids2(shape, 1)
    direct = (row < half) & (lane >= row) | (row >= half) & (lane >= half) & (lane < row)
    full = jnp.where(direct, both, turned)
    spread = jnp.broadcast_to(pltpu.roll(jnp.broadcast_to(diagonal, (8, size)), half, 1)[:1], shape)
    return jnp.where((row >= half) & (row == lane), spread, full)


def packed_shape(count, size):
    pairs = (count + 1) // 2
    return (pairs + (count + size - 1) // size, size, size)


def put_packed(ref, count, index, block):
    size = block.shape[0]
    half = size // 2
    pairs = (count + 1) // 2
    packed, diagonal = pack_block(block)
    second = (index >= pairs).astype(jnp.int32)
    ref[index - second * pairs, pl.ds(pl.multiple_of(second * half, half), half), :] = packed
    ref[pairs + index // size, pl.ds(index % size, 1), :] = diagonal


def get_packed(ref, count, index):
    size = ref.shape[-1]
    half = size // 2
    pairs = (count + 1) // 2
    second = (index >= pairs).astype(jnp.int32)
    packed = ref[index - second * pairs, pl.ds(pl.multiple_of(second * half, half), half), :]
    return unpack_block(packed, ref[pairs + index // size, pl.ds(index % size, 1), :])


def pack_kernel(first_ref, tile_ref, out_ref, *, count):
    def body(r, carry):
        put_packed(out_ref, count, r, tile_ref[first_ref[0] + r])
        return carry

    out_ref[...] = jnp.zeros(out_ref.shape, jnp.float32)
    lax.fori_loop(0, count, body, 0)


def build_kernel(code_ref, tile_ref, *refs):
    arrived, out_ref = refs[:-1], refs[-1]
    room = arrived[0].shape[0]

    def body(r, carry):
        code = code_ref[r]

        @pl.when(code < 0)
        def _():
            out_ref[r] = tile_ref[r]

        for s, ref in enumerate(arrived):

            @pl.when((code >= s * room) & (code < (s + 1) * room))
            def _(s=s, ref=ref):
                out_ref[r] = ref[code - s * room].T

        return carry

    lax.fori_loop(0, out_ref.shape[0], body, 0)


def square_kernel(info_ref, tile_ref, out_ref, *, count):
    def body(r, carry):
        @pl.when(info_ref[1 + r] >= 0)
        def _():
            block = tile_ref[info_ref[0] + r]
            put_packed(out_ref, count, r, split_dot(block, block, ((1,), (1,))))

        return carry

    out_ref[...] = jnp.zeros(out_ref.shape, jnp.float32)
    lax.fori_loop(0, count, body, 0)


def diagonal_kernel(info_ref, tile_ref, left_ref, *refs, count):
    rights, out_ref = refs[:-1], refs[-1]
    first, on_diagonal, layer, layers = info_ref[0], info_ref[1], info_ref[2], len(rights)

    def body(r, carry):
        col = info_ref[4 + r]

        @pl.when((col >= 0) & (on_diagonal == 1))
        def _():
            block = tile_ref[first + r]
            out_ref[r] = split_dot(block, block)

        @pl.when((col >= 0) & (on_diagonal == 0))
        def _():
            block = tile_ref[first + r]
            out_ref[r] = split_dot(get_packed(left_ref, count, r), block)

        for s, ref in enumerate(rights):
            from_layer = lax.rem(layer - s + layers, layers)

            @pl.when((col >= 0) & (on_diagonal == 0) & (lax.div(col, count) == from_layer))
            def _(ref=ref):
                block = tile_ref[first + r]
                right = get_packed(ref, count, lax.rem(col, count))
                out_ref[r] = out_ref[r] + split_dot(block, right)

        return carry

    lax.fori_loop(0, count, body, 0)


def final_kernel(info_ref, base_ref, right_ref, *refs, shifts, count, rows):
    lefts, squares, out_ref = refs[:shifts], refs[shifts:-1], refs[-1]
    begin = pl.program_id(0) * rows

    def body(t, carry):
        r = begin + t
        out_ref[t] = jnp.zeros(out_ref.shape[1:], jnp.float32)
        place = info_ref[r]

        @pl.when(place >= 0)
        def _():
            out_ref[t, place] = base_ref[r]

        @pl.when((place >= 0) & (info_ref[count + 2 * shifts * count + shifts] == 1))
        def _():
            out_ref[t, place] = out_ref[t, place] + sum(
                get_packed(ref, count, r) for ref in squares
            )

        for s in range(shifts):
            at = info_ref[count + 2 * s * count + r]

            @pl.when(at >= 0)
            def _(s=s, at=at):
                q = info_ref[count + (2 * s + 1) * count + r]
                other = info_ref[count + 2 * shifts * count + s]
                product = split_dot(lefts[s][at], right_ref[other, at])
                out_ref[t, q] = out_ref[t, q] + product

        return carry

    lax.fori_loop(0, rows, body, 0)


def call(kernel, out_shape, smem, arrays):
    return pl.pallas_call(
        kernel,
        out_shape=jax.ShapeDtypeStruct(out_shape, jnp.float32),
        in_specs=[SMEM()] + [VMEM() for _ in arrays],
        out_specs=VMEM(),
    )(smem, *arrays)


def per_device(stored_blocks, pattern, result_cols):
    side = lax.axis_size("row")
    layers = lax.axis_size("layer")
    shifts = side - 1
    i, j, l = (lax.axis_index(axis) for axis in AXES)
    own = stored_blocks[0, 0]
    wanted = result_cols[0, 0]
    n, kept = wanted.shape
    size = own.shape[-1]
    h = n // layers
    first = l * h
    swap_room = -(-n * 7 // (12 * layers))
    cross_room = -(-h * 11 // 24)
    ids = jnp.arange(n, dtype=jnp.int32)
    mine_cols = pattern[i, j]
    on_diagonal = i == j
    in_half = (ids >= first) & (ids < first + h)

    def mine_half(values):
        return lax.dynamic_slice_in_dim(values, first, h, axis=-1)

    my_upper = upper_rows(mine_cols, i, j, side)
    my_ranks = ranks(my_upper)
    outgoing = listing(my_upper, my_ranks, ids, swap_room, l * swap_room)
    payload = jnp.take(own, outgoing, axis=0, mode="clip")
    arrived = [send(payload, lambda a, b, c: (b, a, c) if a != b else None)]
    for s in range(1, layers):
        arrived.append(send(arrived[0], lambda a, b, c, s=s: (a, b, (c + s) % layers)))

    packed = call(
        functools.partial(pack_kernel, count=h),
        packed_shape(h, size),
        jnp.reshape(first, (1,)).astype(jnp.int32),
        [own],
    )
    zeros = jnp.zeros_like(packed)
    along_row = [
        send(packed, lambda a, b, c, s=s: (a, (b + s) % side, c) if a == b else None)
        for s in range(1, side)
    ]
    row_diagonal = functools.reduce(jnp.add, along_row)
    up = send(packed, lambda a, b, c: (a + 1, b, c) if a == b and a + 1 < side else None)
    down = send(packed, lambda a, b, c: (a - 1, b, c) if a == b and a > 0 else None)
    held = up + down
    col_diagonal = held
    for s in range(2, side):
        held = send(
            held,
            lambda a, b, c, s=s: (a + 1, b, c)
            if a == b + s - 1 and a + 1 < side
            else ((a - 1, b, c) if a == b - s + 1 and a > 0 else None),
        )
        col_diagonal = col_diagonal + held
    col_diagonals = [col_diagonal] + [
        send(col_diagonal, lambda a, b, c, s=s: (a, b, (c + s) % layers)) for s in range(1, layers)
    ]

    row_wanted = [shifted(wanted, "col", -s) for s in range(1, side)]
    col_wanted = [shifted(wanted, "row", -s) for s in range(1, side)]

    def used_rows(left_cols, right_cols, listed):
        target = pick(right_cols, left_cols)
        return (target >= 0) & jnp.any(listed == target[:, None], axis=1), target

    left_lists, right_lists, counts = [], [], []
    for s in range(1, side):
        to_col = (j + s) % side
        used, _ = used_rows(mine_cols, pattern[j, to_col], row_wanted[s - 1])
        used = used & in_half & ~on_diagonal & (to_col != i)
        left_lists.append(listing(used, ranks(used), ids, cross_room))
        counts.append(jnp.sum(used.astype(jnp.int32)))
        to_row = (i + s) % side
        theirs = pattern[to_row, i]
        used, _ = used_rows(theirs, mine_cols, col_wanted[s - 1])
        used = used & in_half & ~on_diagonal & (to_row != j)
        right_lists.append(listing(used, ranks(used), theirs, cross_room))
        counts.append(jnp.sum(used.astype(jnp.int32)))
    overflow = functools.reduce(jnp.maximum, counts) > cross_room
    tiles_row = jnp.arange(side)[:, None, None]
    tiles_col = jnp.arange(side)[None, :, None]
    all_upper = upper_rows(pattern, tiles_row, tiles_col, side) & (tiles_row != tiles_col)
    overflow = overflow | jnp.any(jnp.sum(all_upper, axis=-1) > layers * swap_room)
    overflow = overflow.astype(jnp.int32).reshape(1)
    for axis in AXES:
        for_axis = [shifted(overflow, axis, s) for s in range(1, lax.axis_size(axis))]
        overflow = functools.reduce(jnp.maximum, for_axis, overflow)

    marks, partners = [], []
    for s in range(1, side):
        middle = (j - s) % side
        used, target = used_rows(pattern[i, middle], pattern[middle, j], wanted)
        used = used & in_half & ~on_diagonal & (middle != i)
        place = jnp.sum(
            jnp.where(wanted == target[:, None], jnp.arange(kept, dtype=jnp.int32), 0), axis=1
        )
        marks.append(mine_half(jnp.where(used, ranks(used), -1)))
        marks.append(mine_half(place))
        partners.append((i - middle) % side - 1)

    their_upper = upper_rows(pattern[j, i], j, i, side)
    their_rank = pick(ranks(their_upper), mine_cols)
    from_layer = their_rank // swap_room
    code = (l - from_layer) % layers * swap_room + their_rank % swap_room
    code = jnp.where(my_upper | (mine_cols < 0), -1, code).astype(jnp.int32)
    tile = call(build_kernel, own.shape, code, [own] + arrived)

    lefts, rights = [], []
    for s in range(1, side):
        right = jnp.take(tile, jnp.maximum(right_lists[s - 1], 0), axis=0, mode="clip")
        rights.append(
            send(
                right,
                lambda a, b, c, s=s: ((a + s) % side, b, c)
                if a != b and (a + s) % side != b
                else None,
            )
        )
        left = jnp.take(tile, left_lists[s - 1], axis=0, mode="clip")
        lefts.append(
            send(
                left,
                lambda a, b, c, s=s: (a, (b + s) % side, c)
                if a != b and (b + s) % side != a
                else None,
            )
        )
    squares = call(
        functools.partial(square_kernel, count=h),
        packed.shape,
        jnp.concatenate([jnp.reshape(first, (1,)), mine_half(mine_cols)]).astype(jnp.int32),
        [tile],
    )
    squares = [
        send(squares, lambda a, b, c, s=s: (a, a, c) if b == (a + s) % side else None)
        for s in range(1, side)
    ]

    hit = (wanted == mine_cols[:, None]) & (mine_cols >= 0)[:, None]
    base_place = jnp.where(
        jnp.any(hit, axis=1),
        jnp.sum(jnp.where(hit, jnp.arange(kept, dtype=jnp.int32), 0), axis=1),
        -1,
    )
    base_place = mine_half(base_place)
    info = jnp.concatenate(
        [
            jnp.stack([first, on_diagonal.astype(jnp.int32), l, l]).astype(jnp.int32),
            jnp.where(base_place >= 0, mine_half(mine_cols), -1),
        ]
    ).astype(jnp.int32)
    base = call(
        functools.partial(diagonal_kernel, count=h),
        (h, size, size),
        info,
        [tile, row_diagonal] + col_diagonals,
    )
    info = jnp.concatenate(
        [base_place]
        + marks
        + [jnp.stack(partners + [on_diagonal.astype(jnp.int32)]).astype(jnp.int32)]
    ).astype(jnp.int32)
    right_stack = jnp.stack(rights)
    rows = next(d for d in range(8, 0, -1) if h % d == 0)

    def finish(info, base, right_stack, lefts, squares, own):
        del own
        arrays = [base, right_stack, *lefts, *squares]
        return pl.pallas_call(
            functools.partial(final_kernel, shifts=shifts, count=h, rows=rows),
            out_shape=jax.ShapeDtypeStruct((h, kept, size, size), jnp.float32),
            grid=(h // rows,),
            in_specs=[SMEM()] + [VMEM() for _ in arrays],
            out_specs=pl.BlockSpec((rows, kept, size, size), lambda t: (t, 0, 0, 0)),
        )(info, *arrays)

    def redo(info, base, right_stack, lefts, squares, own):
        return slow_path(own, pattern, wanted)

    result = lax.cond(overflow[0] > 0, redo, finish, info, base, right_stack, lefts, squares, own)
    return result[None, None]


def solution(mesh):
    return jax.shard_map(
        per_device,
        mesh=mesh,
        in_specs=(P("row", "col", None, None, None), P(), P("row", "col", None, None)),
        out_specs=P("row", "col", "layer", None, None, None),
        check_vma=False,
    )
```

```python
import functools

import jax
import jax.numpy as jnp
from jax import lax
from jax.experimental import pallas as pl
from jax.experimental.pallas import tpu as pltpu
from jax.sharding import PartitionSpec as P

AXES = ("row", "col", "layer")
SMEM = functools.partial(pl.BlockSpec, memory_space=pltpu.SMEM)
VMEM = functools.partial(pl.BlockSpec, memory_space=pltpu.VMEM)
ANY = functools.partial(pl.BlockSpec, memory_space=pl.ANY)


def shifted(value, axis, steps):
    count = lax.axis_size(axis)
    pairs = [(source, (source + steps) % count) for source in range(count)]
    return lax.ppermute(value, axis, pairs)


def accumulate(totals, left_tile, right_tile, left_cols, right_cols, wanted):
    inner_rows = jnp.maximum(left_cols, 0)
    partner = right_tile[inner_rows]
    target = right_cols[inner_rows]
    present = (left_cols >= 0) & (target >= 0)
    products = jnp.einsum(
        "rab,rbc->rac",
        left_tile,
        partner,
        precision=lax.Precision.HIGHEST,
        preferred_element_type=jnp.float32,
    )
    matched = (present[:, None] & (wanted == target[:, None])).astype(jnp.float32)
    return totals + matched[:, :, None, None] * products[:, None]


def complete(stored, mirror_source, pattern, tile_row, tile_col, grid_side):
    col_ids = pattern[tile_row, tile_col]
    safe_cols = jnp.maximum(col_ids, 0)
    local_rows = jnp.arange(stored.shape[0])
    is_upper = local_rows * grid_side + tile_row <= safe_cols * grid_side + tile_col
    mirrored = jnp.swapaxes(mirror_source[safe_cols], 1, 2)
    return jnp.where(is_upper[:, None, None], stored, mirrored)


def slow_path(own_tile, pattern, wanted):
    grid_side = lax.axis_size("row")
    layers = lax.axis_size("layer")
    my_row = lax.axis_index("row")
    my_col = lax.axis_index("col")
    my_layer = lax.axis_index("layer")
    row_count = own_tile.shape[0]
    half = row_count // layers
    mirror = send(own_tile, lambda i, j, l: (j, i, l))
    mirror = jnp.where(my_row == my_col, own_tile, mirror)
    mine = complete(own_tile, mirror, pattern, my_row, my_col, grid_side)
    first = my_layer * half
    mine_wanted = lax.dynamic_slice_in_dim(wanted, first, half)
    totals = jnp.zeros((half, wanted.shape[1]) + own_tile.shape[1:], jnp.float32)

    def step(middle, totals):
        def ring(axis, mine_at):
            def turn(_, held):
                tile, kept, at = held
                kept = jnp.where(at == middle, tile, kept)
                return shifted(tile, axis, -1), kept, (at + 1) % grid_side

            return lax.fori_loop(0, grid_side, turn, (mine, mine, mine_at))[1]

        left = lax.dynamic_slice_in_dim(ring("col", my_col), first, half)
        right = ring("row", my_row)
        left_cols = lax.dynamic_slice_in_dim(pattern[my_row, middle], first, half)
        return accumulate(totals, left, right, left_cols, pattern[middle, my_col], mine_wanted)

    return lax.fori_loop(0, grid_side, step, totals)


def send(value, target):
    rows, cols, layers = (lax.axis_size(axis) for axis in AXES)
    pairs = []
    for i in range(rows):
        for j in range(cols):
            for l in range(layers):
                to = target(i, j, l)
                if to is not None and to != (i, j, l):
                    pairs.append(
                        ((i * cols + j) * layers + l, (to[0] * cols + to[1]) * layers + to[2])
                    )
    return lax.ppermute(value, AXES, pairs)


def pick(table, index):
    ids = jnp.arange(table.shape[-1], dtype=jnp.int32)
    hit = index[..., :, None] == ids
    return jnp.sum(jnp.where(hit, table[..., None, :] + 1, 0), axis=-1) - 1


def ranks(mask):
    ids = jnp.arange(mask.shape[-1], dtype=jnp.int32)
    before = mask[..., None, :] & (ids[None, :] < ids[:, None])
    return jnp.sum(before.astype(jnp.int32), axis=-1)


def listing(mask, order, values, room, start=0):
    slots = jnp.arange(room, dtype=jnp.int32) + start
    hit = mask[..., None, :] & (order[..., None, :] == slots[:, None])
    return jnp.sum(jnp.where(hit, values[..., None, :], 0), axis=-1)


def upper_rows(cols, tile_row, tile_col, grid_side):
    ids = jnp.arange(cols.shape[-1], dtype=jnp.int32)
    return (cols >= 0) & (ids * grid_side + tile_row <= cols * grid_side + tile_col)


def split_dot(left, right, contract=((1,), (0,))):
    left_hi = left.astype(jnp.bfloat16)
    left_lo = (left - left_hi.astype(jnp.float32)).astype(jnp.bfloat16)
    right_hi = right.astype(jnp.bfloat16)
    right_lo = (right - right_hi.astype(jnp.float32)).astype(jnp.bfloat16)

    def dot(a, b):
        return lax.dot_general(a, b, (contract, ((), ())), preferred_element_type=jnp.float32)

    return dot(left_hi, right_hi) + (dot(left_hi, right_lo) + dot(left_lo, right_hi))


def ids2(shape, axis):
    return lax.broadcasted_iota(jnp.int32, shape, axis)


def pack_block(block):
    size = block.shape[0]
    half = size // 2
    shape = (half, size)
    low = pltpu.roll(block[half:], half, 1)
    packed = jnp.where(ids2(shape, 1) < ids2(shape, 0), low, block[:half])
    diagonal = jnp.sum(jnp.where(ids2(shape, 1) == ids2(shape, 0), low, 0.0), axis=0, keepdims=True)
    return packed, diagonal


def unpack_block(packed, diagonal):
    half, size = packed.shape
    shape = (size, size)
    both = jnp.concatenate([packed, pltpu.roll(packed, half, 1)], axis=0)
    turned = both.T
    row, lane = ids2(shape, 0), ids2(shape, 1)
    direct = (row < half) & (lane >= row) | (row >= half) & (lane >= half) & (lane < row)
    full = jnp.where(direct, both, turned)
    spread = jnp.broadcast_to(pltpu.roll(jnp.broadcast_to(diagonal, (8, size)), half, 1)[:1], shape)
    return jnp.where((row >= half) & (row == lane), spread, full)


def packed_shape(count, size):
    pairs = (count + 1) // 2
    return (pairs + (count + size - 1) // size, size, size)


def put_packed(ref, count, index, block):
    size = block.shape[0]
    half = size // 2
    pairs = (count + 1) // 2
    packed, diagonal = pack_block(block)
    second = (index >= pairs).astype(jnp.int32)
    ref[index - second * pairs, pl.ds(pl.multiple_of(second * half, half), half), :] = packed
    ref[pairs + index // size, pl.ds(index % size, 1), :] = diagonal


def get_packed(ref, count, index):
    size = ref.shape[-1]
    half = size // 2
    pairs = (count + 1) // 2
    second = (index >= pairs).astype(jnp.int32)
    packed = ref[index - second * pairs, pl.ds(pl.multiple_of(second * half, half), half), :]
    return unpack_block(packed, ref[pairs + index // size, pl.ds(index % size, 1), :])


def select_kernel(info_ref, tile_ref, direct_ref, relayed_ref, sems, *, side):
    tile_row, tile_col, layer = info_ref[0], info_ref[1], info_ref[2]
    n = tile_ref.shape[0]
    direct, relayed = direct_ref.shape[0], relayed_ref.shape[0]
    start = jnp.where(layer == 0, 0, direct + (layer - 1) * relayed)
    room = jnp.where(layer == 0, direct, relayed)

    def copies(r, slot, action):
        @pl.when((slot >= 0) & (slot < room) & (layer == 0))
        def _():
            action(pltpu.make_async_copy(tile_ref.at[r], direct_ref.at[slot], sems.at[slot]))

        @pl.when((slot >= 0) & (slot < room) & (layer != 0))
        def _():
            action(pltpu.make_async_copy(tile_ref.at[r], relayed_ref.at[slot], sems.at[slot]))

    def sweep(action):
        def body(r, rank):
            col = info_ref[3 + r]
            stored = (col >= 0) & (r * side + tile_row <= col * side + tile_col)
            copies(r, jnp.where(stored, rank - start, -1), action)
            return rank + stored.astype(jnp.int32)

        lax.fori_loop(0, n, body, 0)

    @pl.when(tile_row != tile_col)
    def _():
        sweep(lambda copy: copy.start())
        sweep(lambda copy: copy.wait())


def pack_kernel(info_ref, tile_ref, out_ref, buf_ref, sem, *, count):
    @pl.when(info_ref[1] == 1)
    def _():
        copy = pltpu.make_async_copy(tile_ref.at[pl.ds(info_ref[0], count)], buf_ref, sem)
        copy.start()
        copy.wait()

        def body(r, carry):
            put_packed(out_ref, count, r, buf_ref[r])
            return carry

        lax.fori_loop(0, count, body, 0)


def build_kernel(info_ref, tile_ref, *refs, options, lists, room, cross_room):
    arrived = refs[:options]
    out_ref, list_refs = refs[options], refs[options + 1 : options + 1 + lists]
    buf_ref, sems = refs[options + 1 + lists :]
    n = out_ref.shape[0]
    rows = pltpu.make_async_copy(tile_ref, out_ref, sems.at[options])
    rows.start()
    for o, ref in enumerate(arrived):
        place = info_ref[n + lists * (cross_room + 1) + o]

        @pl.when(place >= 0)
        def _(o=o, ref=ref, place=place):
            at = buf_ref.at[pl.ds(place, ref.shape[0])]
            pltpu.make_async_copy(ref, at, sems.at[o]).start()

    for o, ref in enumerate(arrived):
        place = info_ref[n + lists * (cross_room + 1) + o]

        @pl.when(place >= 0)
        def _(o=o, ref=ref, place=place):
            at = buf_ref.at[pl.ds(place, ref.shape[0])]
            pltpu.make_async_copy(ref, at, sems.at[o]).wait()

    rows.wait()

    def body(r, carry):
        code = info_ref[r]

        @pl.when(code >= 0)
        def _():
            out_ref[r] = buf_ref[code].T

        return carry

    lax.fori_loop(0, n, body, 0)
    for k, ref in enumerate(list_refs):
        base = n + k * (cross_room + 1)

        def move(t, carry, base=base, ref=ref):
            ref[t] = out_ref[info_ref[base + 1 + t]]
            return carry

        lax.fori_loop(0, jnp.minimum(info_ref[base], cross_room), move, 0)


def square_kernel(info_ref, tile_ref, out_ref, *, count):
    def body(r, carry):
        @pl.when(info_ref[1 + r] >= 0)
        def _():
            block = tile_ref[info_ref[0] + r]
            put_packed(out_ref, count, r, split_dot(block, block, ((1,), (1,))))

        return carry

    out_ref[...] = jnp.zeros(out_ref.shape, jnp.float32)
    lax.fori_loop(0, count, body, 0)


def diagonal_kernel(info_ref, tile_ref, left_ref, *refs, count, rows):
    rights, out_ref = refs[:-1], refs[-1]
    on_diagonal, layer, layers = info_ref[1], info_ref[2], len(rights)
    begin = pl.program_id(0) * rows

    def body(t, carry):
        r = begin + t
        col = info_ref[4 + r]
        place = info_ref[4 + count + r]
        out_ref[t] = jnp.zeros(out_ref.shape[1:], jnp.float32)

        @pl.when((place >= 0) & (on_diagonal == 1))
        def _():
            block = tile_ref[t]
            out_ref[t, place] = split_dot(block, block)

        for s, ref in enumerate(rights):
            from_layer = lax.rem(layer - s + layers, layers)

            @pl.when((place >= 0) & (on_diagonal == 0) & (lax.div(col, count) == from_layer))
            def _(ref=ref):
                block = tile_ref[t]
                right = get_packed(ref, count, lax.rem(col, count))
                left = get_packed(left_ref, count, r)
                out_ref[t, place] = split_dot(left, block) + split_dot(block, right)

        return carry

    lax.fori_loop(0, rows, body, 0)


def final_kernel(info_ref, base_ref, *refs, shifts, count, rows):
    lefts, rights = refs[:shifts], refs[shifts : 2 * shifts]
    squares, out_ref = refs[2 * shifts : 3 * shifts], refs[3 * shifts]
    left_buf, right_buf, square_buf, sems = refs[3 * shifts + 1 :]
    begin = pl.program_id(0) * rows
    flags = count + 2 * shifts * count
    on_diagonal = info_ref[flags + 3 * shifts]

    @pl.when(pl.program_id(0) == 0)
    def _():
        moves = []
        for s in range(shifts):
            moves.append((info_ref[flags + shifts + s] == 1, lefts[s], left_buf.at[s]))
            moves.append((info_ref[flags + 2 * shifts + s] == 1, rights[s], right_buf.at[s]))
            moves.append((on_diagonal == 1, squares[s], square_buf.at[s]))
        for k, (wanted, source, target) in enumerate(moves):

            @pl.when(wanted)
            def _(k=k, source=source, target=target):
                pltpu.make_async_copy(source, target, sems.at[k]).start()

        for k, (wanted, source, target) in enumerate(moves):

            @pl.when(wanted)
            def _(k=k, source=source, target=target):
                pltpu.make_async_copy(source, target, sems.at[k]).wait()

        @pl.when(on_diagonal == 1)
        def _():
            for s in range(1, shifts):
                square_buf[0] = square_buf[0] + square_buf[s]

    def body(t, carry):
        r = begin + t
        out_ref[t] = base_ref[t]
        place = info_ref[r]

        @pl.when((place >= 0) & (on_diagonal == 1))
        def _():
            out_ref[t, place] = out_ref[t, place] + get_packed(square_buf.at[0], count, r)

        for s in range(shifts):
            at = info_ref[count + 2 * s * count + r]

            @pl.when(at >= 0)
            def _(s=s, at=at):
                q = info_ref[count + (2 * s + 1) * count + r]
                other = info_ref[flags + s]
                product = split_dot(left_buf[s, at], right_buf[other, at])
                out_ref[t, q] = out_ref[t, q] + product

        return carry

    lax.fori_loop(0, rows, body, 0)


def f32(shape):
    return jax.ShapeDtypeStruct(shape, jnp.float32)


def ints(*parts):
    flat = [jnp.reshape(part, (-1,)).astype(jnp.int32) for part in parts]
    return jnp.concatenate(flat)


def per_device(stored_blocks, pattern, result_cols):
    side = lax.axis_size("row")
    layers = lax.axis_size("layer")
    shifts = side - 1
    i, j, l = (lax.axis_index(axis) for axis in AXES)
    own = stored_blocks[0, 0]
    wanted = result_cols[0, 0]
    n, kept = wanted.shape
    size = own.shape[-1]
    h = n // layers
    first = l * h
    rows = next(d for d in range(8, 0, -1) if h % d == 0)
    swap_room = -(-n * 7 // 12)
    direct_room = swap_room if layers == 1 else -(-swap_room * 4 // 7)
    relayed_room = -(-(swap_room - direct_room) // max(layers - 1, 1))
    swap_room = direct_room + (layers - 1) * relayed_room
    cross_room = -(-h * 11 // 24)
    ids = jnp.arange(n, dtype=jnp.int32)
    mine_cols = pattern[i, j]
    on_diagonal = i == j
    diagonal_flag = on_diagonal.astype(jnp.int32)
    in_half = (ids >= first) & (ids < first + h)

    def mine_half(values):
        return lax.dynamic_slice_in_dim(values, first, h, axis=-1)

    direct, relayed = pl.pallas_call(
        functools.partial(select_kernel, side=side),
        out_shape=[f32((direct_room, size, size)), f32((relayed_room, size, size))],
        in_specs=[SMEM(), ANY()],
        out_specs=[ANY(), ANY()],
        scratch_shapes=[pltpu.SemaphoreType.DMA((max(direct_room, relayed_room),))],
    )(ints(i, j, l, mine_cols), own)
    direct, relayed, own_later, wanted_later, pattern = lax.optimization_barrier(
        (direct, relayed, own, wanted, pattern)
    )
    swapped = send(direct, lambda a, b, c: (b, a, c) if a != b and c == 0 else None)
    hops = [
        send(relayed, lambda a, b, c, s=s: (a, a, c) if b == (a + s) % side and c else None)
        for s in range(1, side)
    ]
    hops = [
        send(hop, lambda a, b, c, s=s: ((a + s) % side, a, c) if a == b and c else None)
        for s, hop in enumerate(hops, 1)
    ]
    parts = [(swapped, l == 0, 0)]
    for c in range(1, layers):
        parts.append(
            (send(swapped, lambda a, b, e, c=c: (a, b, c) if a != b and e == 0 else None), l == c, 0)
        )
    for s, hop in enumerate(hops, 1):
        here = (i - j) % side == s
        parts.append((hop, here & (l > 0), direct_room + (l - 1) * relayed_room))
        for c in range(1, layers):
            moved = send(
                hop,
                lambda a, b, e, c=c, s=s: (a, b, (e + c) % layers)
                if (a - b) % side == s and e
                else None,
            )
            source = (l - c) % layers
            parts.append((moved, here & (source > 0), direct_room + (source - 1) * relayed_room))

    packed = pl.pallas_call(
        functools.partial(pack_kernel, count=h),
        out_shape=f32(packed_shape(h, size)),
        in_specs=[SMEM(), ANY()],
        out_specs=VMEM(),
        scratch_shapes=[pltpu.VMEM((h, size, size), jnp.float32), pltpu.SemaphoreType.DMA(())],
    )(ints(first, diagonal_flag), own_later)
    bits = [1 << b for b in range(side.bit_length() - 1)]
    row_diagonal = packed
    away = i ^ j
    for t in range(len(bits)):
        def onward(a, b, c, t=t):
            order = bits if c % 2 == 0 else bits[::-1]
            return (a, b ^ order[t], c) if (a ^ b) & ~sum(order[:t]) == 0 else None

        came = send(row_diagonal, onward)
        bit = jnp.where(l % 2 == 0, bits[t], bits[::-1][t])
        row_diagonal = jnp.where((away & bit) != 0, came, row_diagonal)
    up = send(packed, lambda a, b, c: (a + 1, b, c) if a == b and a + 1 < side else None)
    down = send(packed, lambda a, b, c: (a - 1, b, c) if a == b and a > 0 else None)
    held = jnp.where(i > j, up, down)
    col_diagonal = held
    for s in range(2, side):
        held = send(
            held,
            lambda a, b, c, s=s: (a + 1, b, c)
            if a == b + s - 1 and a + 1 < side
            else ((a - 1, b, c) if a == b - s + 1 and a > 0 else None),
        )
        col_diagonal = jnp.where(jnp.abs(i - j) == s, held, col_diagonal)
    col_diagonals = [col_diagonal] + [
        send(
            col_diagonal,
            lambda a, b, c, s=s: (a, b, (c + s) % layers) if a != b else None,
        )
        for s in range(1, layers)
    ]

    row_wanted = [shifted(wanted_later, "col", -s) for s in range(1, side)]
    col_wanted = [shifted(wanted_later, "row", -s) for s in range(1, side)]

    def used_rows(left_cols, right_cols, listed):
        target = pick(right_cols, left_cols)
        return (target >= 0) & jnp.any(listed == target[:, None], axis=1), target

    listings, counts = [], []
    for s in range(1, side):
        to_row = (i + s) % side
        theirs = pattern[to_row, i]
        used, _ = used_rows(theirs, mine_cols, col_wanted[s - 1])
        used = used & in_half & ~on_diagonal & (to_row != j)
        counts.append(jnp.sum(used.astype(jnp.int32)))
        listings.append(ints(counts[-1], listing(used, ranks(used), theirs, cross_room)))
        to_col = (j + s) % side
        used, _ = used_rows(mine_cols, pattern[j, to_col], row_wanted[s - 1])
        used = used & in_half & ~on_diagonal & (to_col != i)
        counts.append(jnp.sum(used.astype(jnp.int32)))
        listings.append(ints(counts[-1], listing(used, ranks(used), ids, cross_room)))
    overflow = functools.reduce(jnp.maximum, counts) > cross_room
    tiles_row = jnp.arange(side)[:, None, None]
    tiles_col = jnp.arange(side)[None, :, None]
    all_upper = upper_rows(pattern, tiles_row, tiles_col, side) & (tiles_row != tiles_col)
    overflow = overflow | jnp.any(jnp.sum(all_upper, axis=-1) > swap_room)
    overflow = overflow.astype(jnp.int32).reshape(1)
    for axis in AXES:
        for_axis = [shifted(overflow, axis, s) for s in range(1, lax.axis_size(axis))]
        overflow = functools.reduce(jnp.maximum, for_axis, overflow)

    marks, partners = [], []
    for s in range(1, side):
        middle = (j - s) % side
        used, target = used_rows(pattern[i, middle], pattern[middle, j], wanted_later)
        used = used & in_half & ~on_diagonal & (middle != i)
        place = jnp.sum(
            jnp.where(wanted_later == target[:, None], jnp.arange(kept, dtype=jnp.int32), 0), axis=1
        )
        marks.append(mine_half(jnp.where(used, ranks(used), -1)))
        marks.append(mine_half(place))
        partners.append((i - middle) % side - 1)
    hit = (wanted_later == mine_cols[:, None]) & (mine_cols >= 0)[:, None]
    base_place = jnp.where(
        jnp.any(hit, axis=1),
        jnp.sum(jnp.where(hit, jnp.arange(kept, dtype=jnp.int32), 0), axis=1),
        -1,
    )
    base_place = mine_half(base_place)
    left_valid = [~on_diagonal & ((j - s) % side != i) for s in range(1, side)]
    right_valid = [~on_diagonal & ((i - s) % side != j) for s in range(1, side)]
    final_info = ints(
        base_place, *marks, *partners, *left_valid, *right_valid, diagonal_flag
    )
    base_info = ints(first // rows, diagonal_flag, l, l, mine_half(mine_cols), base_place)
    square_info = ints(first, mine_half(mine_cols))

    their_upper = upper_rows(pattern[j, i], j, i, side)
    their_rank = pick(ranks(their_upper), mine_cols)
    my_upper = upper_rows(mine_cols, i, j, side)
    code = jnp.where(my_upper | (their_rank >= swap_room), -1, their_rank)
    places = [jnp.where(valid & ~on_diagonal, place, -1) for _, valid, place in parts]
    build_info = ints(code, *listings, *places)
    build_info, overflow, final_info, base_info, square_info = lax.optimization_barrier(
        (build_info, overflow, final_info, base_info, square_info)
    )
    arrays = [part for part, _, _ in parts]
    built = pl.pallas_call(
        functools.partial(
            build_kernel,
            options=len(arrays),
            lists=2 * shifts,
            room=swap_room,
            cross_room=cross_room,
        ),
        out_shape=[f32(own.shape)] + [f32((cross_room, size, size))] * (2 * shifts),
        in_specs=[SMEM(), ANY()] + [ANY() for _ in arrays],
        out_specs=[VMEM()] * (1 + 2 * shifts),
        scratch_shapes=[
            pltpu.VMEM((swap_room, size, size), jnp.float32),
            pltpu.SemaphoreType.DMA((len(arrays) + 1,)),
        ],
    )(build_info, own_later, *arrays)
    tile = built[0]
    lefts, rights = [], []
    for s in range(1, side):
        rights.append(
            send(
                built[2 * s - 1],
                lambda a, b, c, s=s: ((a + s) % side, b, c)
                if a != b and (a + s) % side != b
                else None,
            )
        )
        lefts.append(
            send(
                built[2 * s],
                lambda a, b, c, s=s: (a, (b + s) % side, c)
                if a != b and (b + s) % side != a
                else None,
            )
        )
    squares = pl.pallas_call(
        functools.partial(square_kernel, count=h),
        out_shape=f32(packed.shape),
        in_specs=[SMEM(), VMEM()],
        out_specs=VMEM(),
    )(square_info, tile)
    squares = [
        send(squares, lambda a, b, c, s=s: (a, a, c) if b == (a + s) % side else None)
        for s in range(1, side)
    ]
    base = pl.pallas_call(
        functools.partial(diagonal_kernel, count=h, rows=rows),
        out_shape=f32((h, kept, size, size)),
        grid_spec=pltpu.PrefetchScalarGridSpec(
            num_scalar_prefetch=1,
            grid=(h // rows,),
            in_specs=[pl.BlockSpec((rows, size, size), lambda t, info: (info[0] + t, 0, 0)), VMEM()]
            + [VMEM() for _ in col_diagonals],
            out_specs=pl.BlockSpec((rows, kept, size, size), lambda t, info: (t, 0, 0, 0)),
        ),
    )(base_info, tile, row_diagonal, *col_diagonals)

    def finish(info, base, lefts, rights, squares, own):
        del own
        arrays = [*lefts, *rights, *squares]
        cross = (shifts, cross_room, size, size)
        return pl.pallas_call(
            functools.partial(final_kernel, shifts=shifts, count=h, rows=rows),
            out_shape=f32((h, kept, size, size)),
            grid=(h // rows,),
            in_specs=[SMEM(), pl.BlockSpec((rows, kept, size, size), lambda t: (t, 0, 0, 0))]
            + [ANY() for _ in arrays],
            out_specs=pl.BlockSpec((rows, kept, size, size), lambda t: (t, 0, 0, 0)),
            scratch_shapes=[
                pltpu.VMEM(cross, jnp.float32),
                pltpu.VMEM(cross, jnp.float32),
                pltpu.VMEM((shifts,) + packed.shape, jnp.float32),
                pltpu.SemaphoreType.DMA((3 * shifts,)),
            ],
        )(info, base, *arrays)

    def redo(info, base, lefts, rights, squares, own):
        return slow_path(own, pattern, wanted)

    result = lax.cond(overflow[0] > 0, redo, finish, final_info, base, lefts, rights, squares, own)
    return result[None, None]


def solution(mesh):
    return jax.shard_map(
        per_device,
        mesh=mesh,
        in_specs=(P("row", "col", None, None, None), P(), P("row", "col", None, None)),
        out_specs=P("row", "col", "layer", None, None, None),
        check_vma=False,
    )
```
